256 devices in a mesh: row: 8 (over x, core), col: 32 (over z, y).
Axes of the slice: x: 4, y: 4, z: 8, core: 2. Of those that a mesh axis runs over, the one named last changes fastest.
Arguments:
- features: float32 [32768, 512], P(('col', 'row')), may hold values from -6 to 6
- weight: float32 [512, 512], replicated, may hold values from -0.25 to 0.25
- cotangent: bfloat16 [32768, 512], P(('row', 'col')), may hold values from -6 to 6
- block_values: bfloat16 [8, 32, 96, 128, 128], P('row', 'col'), may hold values from -0.0625 to 0.0625
- block_coords: int32 [8, 32, 2, 96], P('row', 'col'), may hold values from -1 to 31, as said below
Outputs:
- activated: float32 [32768, 512], P(('row', 'col'))
- dfeatures: float32 [32768, 512], P(('col', 'row'))
- dweight: float32 [512, 512], P('row', 'col')
The draws below stay inside these ranges and needn't reach their ends.
Inputs may be any that keep to these rules, and one draw needn't show every extreme that they name: block_coords[r, c, 0, s] is a block row below 32 and block_coords[r, c, 1, s] a block column below 8 of slot s of device (r, c), or both are -1 for an unused slot. Used slots come first and name distinct blocks; each device uses between a quarter of 96 (rounded down) and all 96 slots, and some device uses all 96.
All inputs are finite; a program needn't handle non-finite values.
Results may differ from the reference program's by a relative error of at most 0.006.
Values may be sent and summed in bfloat16 or wider, within the bound.
No kernel may reach another device: no remote copies, remote signals or barrier semaphores. Data moves between devices by JAX's collectives and lax.ppermute only.
A program may use at most 128 MiB of HBM per device.

```python
import jax
import jax.numpy as jnp
from jax import lax

HID = 512
BLK = 128
ROWS_DEV = 128
NODES = 32768
RBLOCKS = 32
CBLOCKS = 8
NB = 96
N_ROW = 8
N_COL = 32


def draw_block_coords(key, part):
    base_key = jax.random.fold_in(key, 7)
    key_count, key_full, key_order = jax.random.split(base_key, 3)
    device_total = N_ROW * N_COL
    slot_total = RBLOCKS * CBLOCKS
    live_count = jax.random.randint(key_count, (device_total,), NB // 4, NB + 1)
    full_device = jax.random.randint(key_full, (), 0, device_total)
    live_count = jnp.where(jnp.arange(device_total) == full_device, NB, live_count)
    order_keys = jax.random.split(key_order, device_total)
    chosen = jax.vmap(lambda single: jax.random.permutation(single, slot_total)[:NB])(order_keys)
    live_slots = jnp.arange(NB)[None, :] < live_count[:, None]
    row_ids = jnp.where(live_slots, chosen // CBLOCKS, -1)
    col_ids = jnp.where(live_slots, chosen % CBLOCKS, -1)
    return jnp.stack([row_ids, col_ids], axis=1).reshape(N_ROW, N_COL, 2, NB).astype(jnp.int32)


def block_levels(key, extent, shards, low, top_value):
    level, own = 1.0, jax.random.fold_in(key, 6)
    for dim, blocks in shards:
        heights = jnp.exp(jax.random.uniform(jax.random.fold_in(own, dim), (blocks,), jnp.float32, low / len(shards), top_value / len(shards)))
        level = level * jnp.repeat(heights, extent[dim] // blocks).reshape([-1 if axis == dim else 1 for axis in range(len(extent))])
    return level


def gaussian(rng, dims, spread, reach, shards=(), kind=jnp.bfloat16):
    result = spread * jax.random.normal(rng, dims, jnp.float32)
    if shards:
        result = result * block_levels(rng, dims, shards, -0.22, 0.18)
    return jnp.clip(result, -reach, reach).astype(kind)


def setup_inputs(seed: int = 0) -> dict:
    arg_keys = jax.random.split(jax.random.key(seed), 6)
    features = gaussian(arg_keys[0], (NODES, HID), 1.0, 6.0, ((0, 256),), jnp.float32)
    weight = gaussian(arg_keys[1], (HID, HID), HID ** -0.5, 0.25, (), jnp.float32)
    cotangent = gaussian(arg_keys[2], (NODES, HID), 1.0, 6.0, ((0, 256),))
    block_values = gaussian(arg_keys[3], (N_ROW, N_COL, NB, BLK, BLK), (N_ROW * N_COL * ROWS_DEV // 4) ** -0.5, 0.0625, ((0, 8), (1, 32)))
    block_coords = draw_block_coords(jax.random.fold_in(arg_keys[5], 71), 0)
    return {"features": features, "weight": weight, "cotangent": cotangent, "block_values": block_values, "block_coords": block_coords}


def silu_slope(values):
    sigma = jax.nn.sigmoid(values)
    return sigma * (1.0 + values * (1.0 - sigma))


def forward_tile(slot_values, coordinate, tile_stack):
    slot_rows = coordinate[0]
    slot_cols = coordinate[1]
    live_slots = slot_rows >= 0
    masked = jnp.where(live_slots[:, None, None], slot_values.astype(jnp.float32), jnp.float32(0.0))
    selected = tile_stack[jnp.maximum(slot_cols, 0).astype(jnp.int32)].astype(jnp.float32)
    products = jnp.einsum("sab,sbc->sac", masked, selected)
    return jax.ops.segment_sum(products, jnp.maximum(slot_rows, 0).astype(jnp.int32), num_segments=RBLOCKS)


def backward_tile(slot_values, coordinate, tile_stack):
    slot_rows = coordinate[0]
    slot_cols = coordinate[1]
    live_slots = slot_rows >= 0
    masked = jnp.where(live_slots[:, None, None], slot_values.astype(jnp.float32), jnp.float32(0.0))
    selected = tile_stack[jnp.maximum(slot_rows, 0).astype(jnp.int32)].astype(jnp.float32)
    products = jnp.einsum("sab,sac->sbc", masked, selected)
    return jax.ops.segment_sum(products, jnp.maximum(slot_cols, 0).astype(jnp.int32), num_segments=CBLOCKS)


def reference(features, weight, cotangent, block_values, block_coords):
    xcopy = features.astype(jnp.bfloat16)
    wcopy = weight.astype(jnp.bfloat16)
    projected = jnp.dot(xcopy, wcopy, preferred_element_type=jnp.float32).astype(jnp.bfloat16)
    column_tiles = projected.reshape(N_COL, CBLOCKS, BLK, HID)

    def row_range(row_index):
        def add_device(totals, col_index):
            term = forward_tile(block_values[row_index, col_index], block_coords[row_index, col_index], column_tiles[col_index])
            return totals + term, None

        zero_sums = jnp.zeros((RBLOCKS, BLK, HID), jnp.float32)
        totals, _ = lax.scan(add_device, zero_sums, jnp.arange(N_COL, dtype=jnp.int32))
        return totals

    aggregate = lax.map(row_range, jnp.arange(N_ROW, dtype=jnp.int32)).reshape(NODES, HID)
    activated = jax.nn.silu(aggregate)
    slope = (cotangent.astype(jnp.float32) * silu_slope(aggregate)).astype(jnp.bfloat16)
    row_tiles = slope.reshape(N_ROW, RBLOCKS, BLK, HID)

    def column_range(col_index):
        def add_device(totals, row_index):
            term = backward_tile(block_values[row_index, col_index], block_coords[row_index, col_index], row_tiles[row_index])
            return totals + term, None

        zero_sums = jnp.zeros((CBLOCKS, BLK, HID), jnp.float32)
        totals, _ = lax.scan(add_device, zero_sums, jnp.arange(N_ROW, dtype=jnp.int32))
        return totals

    node_grad = lax.map(column_range, jnp.arange(N_COL, dtype=jnp.int32)).reshape(NODES, HID)
    grad_copy = node_grad.astype(jnp.bfloat16)
    dfeatures = jnp.dot(grad_copy, wcopy.T, preferred_element_type=jnp.float32)
    dweight = jnp.dot(xcopy.T, grad_copy, preferred_element_type=jnp.float32) * (1.0 / NODES ** 0.5)
    return activated, dfeatures, dweight
```

```python
import jax
import jax.numpy as jnp
from jax import lax
from jax.experimental import pallas as pl
from jax.experimental.pallas import tpu as pltpu
from jax.sharding import PartitionSpec as P

HID = 512
BLK = 128
NB = 96
NX, NC, NZ, NY = 4, 2, 8, 4
HALF = BLK // 2
F32 = jnp.float32
BF16 = jnp.bfloat16


def shift(value, axis, step):
    if axis == "z":
        return lax.ppermute(
            value, "col", [(i, (i // NY + step) % NZ * NY + i % NY) for i in range(NZ * NY)]
        )
    if axis == "y":
        return lax.ppermute(
            value, "col", [(i, i // NY * NY + (i % NY + step) % NY) for i in range(NZ * NY)]
        )
    if axis == "x":
        return lax.ppermute(
            value, "row", [(i, (i // NC + step) % NX * NC + i % NC) for i in range(NX * NC)]
        )
    return lax.ppermute(value, "row", [(i, i ^ 1) for i in range(NX * NC)])


def ring_sum(chunks, axis):
    count = len(chunks)
    far = count // 2
    cut = chunks[0].shape[0] // 2
    right = shift(chunks[far][:cut].astype(BF16), axis, 1)
    left = shift(chunks[far][cut:].astype(BF16), axis, -1)
    for d in range(far - 1, 0, -1):
        ahead, behind = chunks[d].astype(F32), chunks[count - d].astype(F32)
        if d == far - 1:
            ahead = jnp.concatenate([ahead[:cut] + right.astype(F32), ahead[cut:]], 0)
            behind = jnp.concatenate([behind[:cut], behind[cut:] + left.astype(F32)], 0)
        else:
            ahead = ahead + right.astype(F32)
            behind = behind + left.astype(F32)
        right = shift(ahead.astype(BF16), axis, 1)
        left = shift(behind.astype(BF16), axis, -1)
    return chunks[0].astype(F32) + right.astype(F32) + left.astype(F32)


def ring_gather(own, axis, count):
    far = count // 2
    cut = own.shape[0] // 2
    pieces = [None] * count
    pieces[0] = own
    right = left = own
    for step in range(1, far):
        right = shift(right, axis, 1)
        left = shift(left, axis, -1)
        pieces[count - step] = right
        pieces[step] = left
    pieces[far] = (shift(right[:cut], axis, 1), shift(left[cut:], axis, -1))
    return pieces


def joined(pieces):
    flat = []
    for piece in pieces:
        flat.extend(piece if isinstance(piece, tuple) else (piece,))
    return jnp.concatenate(flat, 0)


def fill_tiles(tile_ref, slots, vals_ref, lhs_ref, where):
    for (row, col), slot in zip(where, slots):
        tile = vals_ref[jnp.minimum(slot, NB - 1)]
        lhs_ref[row * BLK : (row + 1) * BLK, col * BLK : (col + 1) * BLK] = jnp.where(
            slot < NB, tile, jnp.zeros_like(tile)
        )


def forward_kernel(table, xa, xb, w, vals, y0, y1, y2, y3, zo, projected, lhs):
    turn = pl.program_id(0)

    @pl.when(turn == 0)
    def _():
        half = xa.shape[0]
        projected[:half] = jnp.dot(xa[...], w[...], preferred_element_type=F32).astype(BF16)
        projected[half:] = jnp.dot(xb[...], w[...], preferred_element_type=F32).astype(BF16)

    where = [(k, j) for k in range(NY) for j in range(NX * NC)]
    slots = [table[(turn * NY + k) * NX * NC + j] for k, j in where]
    fill_tiles(table, slots, vals, lhs, where)
    out = jnp.dot(lhs[...], projected[...], preferred_element_type=F32).astype(BF16)
    for k, y in enumerate((y0, y1, y2, y3)):
        y[0] = out[k * BLK : k * BLK + HALF]
        zo[0, k] = out[k * BLK + HALF : (k + 1) * BLK]


def forward_blocks(table, xa, xb, w, vals):
    full = lambda *shape: pl.BlockSpec(shape, lambda g, t: (0,) * len(shape))
    yspec = pl.BlockSpec((1, HALF, HID), lambda g, t: (g, 0, 0))
    return pl.pallas_call(
        forward_kernel,
        grid_spec=pltpu.PrefetchScalarGridSpec(
            num_scalar_prefetch=1,
            grid=(NZ,),
            in_specs=[
                full(NX * BLK, HID),
                full(NX * BLK, HID),
                full(HID, HID),
                full(NB, BLK, BLK),
            ],
            out_specs=[yspec] * NY + [pl.BlockSpec((1, NY, HALF, HID), lambda g, t: (g, 0, 0, 0))],
            scratch_shapes=[
                pltpu.VMEM((NX * NC * BLK, HID), BF16),
                pltpu.VMEM((NY * BLK, NX * NC * BLK), BF16),
            ],
        ),
        out_shape=[jax.ShapeDtypeStruct((NZ, HALF, HID), BF16)] * NY
        + [jax.ShapeDtypeStruct((NZ, NY, HALF, HID), BF16)],
        compiler_params=pltpu.CompilerParams(vmem_limit_bytes=40 << 20),
        name="forward_blocks",
    )(table, xa, xb, w, vals)


def backward_kernel(table, place, vals, xt, *rest):
    pieces = rest[:14]
    near, away, slope, acc, lhs, dw, sems = rest[14:]
    turn = pl.program_id(0)
    zcut, ycut = NZ // 2, NY // 2

    @pl.when(turn == 0)
    def _():
        lower, upper = pl.ds(0, HALF), pl.ds(HALF, HALF)
        y0, y1, y2a, y2b, y3, z0, z1, z2, z3, z4a, z4b, z5, z6, z7 = pieces
        moves = [
            (y0, slope.at[:, 0, lower]),
            (y1, slope.at[:, 1, lower]),
            (y2a, slope.at[pl.ds(0, zcut), 2, lower]),
            (y2b, slope.at[pl.ds(zcut, zcut), 2, lower]),
            (y3, slope.at[:, 3, lower]),
            (z4a, slope.at[4, pl.ds(0, ycut), upper]),
            (z4b, slope.at[4, pl.ds(ycut, ycut), upper]),
        ]
        for k, z in zip((0, 1, 2, 3, 5, 6, 7), (z0, z1, z2, z3, z5, z6, z7)):
            moves.append((z, slope.at[k, :, upper]))
        copies = [
            pltpu.make_async_copy(src, dst, sems.at[k]) for k, (src, dst) in enumerate(moves)
        ]
        for copy in copies:
            copy.start()
        acc[...] = jnp.zeros_like(acc)
        for copy in copies:
            copy.wait()

    where = [(j, k) for j in range(NX * NC) for k in range(NY)]
    slots = [table[(turn * NY + k) * NX * NC + j] for j, k in where]
    fill_tiles(table, slots, vals, lhs, where)
    acc[...] += jnp.dot(
        lhs[...], slope[turn].reshape(NY * BLK, HID), preferred_element_type=F32
    )

    @pl.when(turn == NZ - 1)
    def _():
        dw[...] = jnp.dot(xt[...], acc[...].astype(BF16), preferred_element_type=F32)
        part = HID // (NX * NC)
        for xr in range(NX):
            x = lax.rem(place[0] + xr, NX)
            near[xr, :BLK] = acc[xr * BLK : (xr + 1) * BLK]
            near[xr, BLK:] = dw[pl.ds((x * NC + place[1]) * part, part)]
            away[xr, :BLK] = acc[(NX + xr) * BLK : (NX + xr + 1) * BLK].astype(BF16)
            away[xr, BLK:] = dw[pl.ds((x * NC + 1 - place[1]) * part, part)].astype(BF16)


def backward_blocks(table, place, vals, xt, pieces):
    full = lambda *shape: pl.BlockSpec(shape, lambda g, t, p: (0,) * len(shape))
    deep = BLK + HID // (NX * NC)
    return pl.pallas_call(
        backward_kernel,
        grid_spec=pltpu.PrefetchScalarGridSpec(
            num_scalar_prefetch=2,
            grid=(NZ,),
            in_specs=[full(NB, BLK, BLK), full(HID, NX * NC * BLK)]
            + [pl.BlockSpec(memory_space=pl.ANY)] * len(pieces),
            out_specs=[full(NX, deep, HID), full(NX, deep, HID)],
            scratch_shapes=[
                pltpu.VMEM((NZ, NY, BLK, HID), BF16),
                pltpu.VMEM((NX * NC * BLK, HID), F32),
                pltpu.VMEM((NX * NC * BLK, NY * BLK), BF16),
                pltpu.VMEM((HID, HID), F32),
                pltpu.SemaphoreType.DMA((len(pieces),)),
            ],
        ),
        out_shape=[
            jax.ShapeDtypeStruct((NX, deep, HID), F32),
            jax.ShapeDtypeStruct((NX, deep, HID), BF16),
        ],
        compiler_params=pltpu.CompilerParams(vmem_limit_bytes=40 << 20),
        name="backward_blocks",
    )(table, place, vals, xt, *pieces)


def on_device(features, weight, cotangent, block_values, block_coords):
    values = block_values[0, 0]
    coords = block_coords[0, 0]
    row = lax.axis_index("row")
    col = lax.axis_index("col")
    x, core = row // NC, row % NC
    z, y = col // NY, col % NY

    xcopy = features.astype(BF16)
    wcopy = weight.astype(BF16)
    xa = joined(ring_gather(xcopy, "x", NX))
    xb = shift(xa, "core", 1)

    zr = lax.rem(coords[0] // NY - z + NZ, NZ)
    yr = lax.rem(coords[0] % NY - y + NY, NY)
    xr = lax.rem(coords[1] // NC - x + NX, NX)
    cr = lax.rem(coords[1] % NC - core + NC, NC)
    key = jnp.where(coords[0] >= 0, (zr * NY + yr) * (NX * NC) + cr * NX + xr, -1)
    spots = lax.broadcasted_iota(jnp.int32, (NZ * NY * NX * NC, NB), 0)
    slot_ids = lax.broadcasted_iota(jnp.int32, (NZ * NY * NX * NC, NB), 1)
    table = jnp.min(jnp.where(spots == key[None, :], slot_ids, NB), axis=1)

    y0, y1, y2, y3, zo = forward_blocks(table, xa, xb, wcopy, values)
    by_y = ring_sum([y0, y1, y2, y3], "y").astype(BF16)
    by_z = ring_sum([zo[k] for k in range(NZ)], "z").astype(BF16)
    top = ring_sum([by_y[k] for k in range(NZ)], "z")
    bottom = ring_sum([by_z[k] for k in range(NY)], "y")

    def slope_of(total, cot):
        sigma = jax.nn.sigmoid(total)
        slope = cot.astype(F32) * sigma * (1.0 + total * (1.0 - sigma))
        return total * sigma, slope.astype(BF16)

    top_active, top_slope = slope_of(top, cotangent[:HALF])
    bottom_active, bottom_slope = slope_of(bottom, cotangent[HALF:])
    activated = jnp.concatenate([top_active, bottom_active], 0)

    top_all = joined(ring_gather(top_slope, "z", NZ)).reshape(NZ, HALF, HID)
    bottom_all = joined(ring_gather(bottom_slope, "y", NY)).reshape(NY, HALF, HID)
    ypieces = ring_gather(top_all, "y", NY)
    zpieces = ring_gather(bottom_all, "z", NZ)
    pieces = [ypieces[0], ypieces[1], *ypieces[2], ypieces[3]]
    pieces += [*zpieces[:4], *zpieces[4], *zpieces[5:]]

    xt = jnp.concatenate([xa, xb], 0).T
    place = jnp.stack([x, core]).astype(jnp.int32)
    near, away = backward_blocks(table, place, values.swapaxes(1, 2), xt, pieces)
    both = near + shift(away, "core", 1).astype(F32)
    total = ring_sum([both[k] for k in range(NX)], "x")
    grad_copy = total[:BLK].astype(BF16)
    dfeatures = lax.dot_general(
        grad_copy, wcopy, (((1,), (1,)), ((), ())), preferred_element_type=F32
    )
    part, width = HID // (NX * NC), HID // (NZ * NY)
    rows = total[BLK:].reshape(part, NZ * NY, width).swapaxes(0, 1)
    rows = rows.reshape(NZ * NY, part * width // 128, 128)
    shares = lax.all_to_all(rows, "col", 0, 0, tiled=True)
    node_total = BLK * NX * NC * NZ * NY
    dweight = jnp.sum(shares, axis=0).reshape(part, width) * (1.0 / node_total**0.5)
    return activated, dfeatures, dweight


def solution(mesh):
    placed = (
        P(("col", "row"), None),
        P(),
        P(("row", "col"), None),
        P("row", "col", None, None, None),
        P("row", "col", None, None),
    )
    return jax.shard_map(
        on_device,
        mesh=mesh,
        in_specs=placed,
        out_specs=(P(("row", "col"), None), P(("col", "row"), None), P("row", "col")),
        check_vma=False,
    )
```

```python
import jax
import jax.numpy as jnp
from jax import lax
from jax.experimental import pallas as pl
from jax.experimental.pallas import tpu as pltpu
from jax.sharding import PartitionSpec as P

HID = 512
BLK = 128
NB = 96
NX, NC, NZ, NY = 4, 2, 8, 4
HALF = BLK // 2
TOP = 80
PIECES = 2
F32 = jnp.float32
BF16 = jnp.bfloat16


def shift(value, axis, step):
    if axis == "z":
        return lax.ppermute(
            value, "col", [(i, (i // NY + step) % NZ * NY + i % NY) for i in range(NZ * NY)]
        )
    if axis == "y":
        return lax.ppermute(
            value, "col", [(i, i // NY * NY + (i % NY + step) % NY) for i in range(NZ * NY)]
        )
    if axis == "x":
        return lax.ppermute(
            value, "row", [(i, (i // NC + step) % NX * NC + i % NC) for i in range(NX * NC)]
        )
    return lax.ppermute(value, "row", [(i, i ^ 1) for i in range(NX * NC)])


def ring_sum(chunks, axis, cut=None, wire=BF16):
    count = len(chunks)
    far = count // 2
    cut = cut or chunks[0].shape[0] // 2

    def both_ways(right, left):
        right = shift(right.astype(wire), axis, 1).astype(F32)
        left = shift(left.astype(wire), axis, -1).astype(F32)
        return right, left

    right, left = both_ways(chunks[far][:cut], chunks[far][cut:])
    for d in range(far - 1, 0, -1):
        ahead, behind = chunks[d].astype(F32), chunks[count - d].astype(F32)
        if d == far - 1:
            ahead = jnp.concatenate([ahead[:cut] + right, ahead[cut:]], 0)
            behind = jnp.concatenate([behind[:cut], behind[cut:] + left], 0)
        else:
            ahead = ahead + right
            behind = behind + left
        right, left = both_ways(ahead, behind)
    own = chunks[0].astype(F32)
    return own + right + left


def ring_gather(own, axis, count):
    pieces = [None] * count
    pieces[0] = right = left = own
    for step in range(1, count // 2 + 1):
        right = shift(right, axis, 1)
        pieces[count - step] = right
        if step < count - step:
            left = shift(left, axis, -1)
            pieces[step] = left
    return pieces


def fill_tile(slot, vals_ref, lhs_ref, row, col):
    tile = vals_ref[jnp.minimum(slot, NB - 1)]
    lhs_ref[pl.ds(row, BLK), pl.ds(col, BLK)] = jnp.where(
        slot < NB, tile, jnp.zeros_like(tile)
    )


def whole(*shape):
    return pl.BlockSpec(shape, lambda *_: (0,) * len(shape), pipeline_mode=pl.Buffered(1))


def forward_kernel(table, place, vals, *rest):
    pieces = rest[:PIECES]
    y0, y1, y2, y3, zo, gathered, lhs, sems = rest[PIECES:]
    turn = pl.program_id(0)

    def tile_rows(turn):
        for k in range(NY):
            for j in range(NX * NC):
                slot = table[(turn * NY + k) * NX * NC + j]
                fill_tile(slot, vals, lhs, k * BLK, j * BLK)

    @pl.when(turn == 0)
    def _():
        copies, start = [], 0
        for k, piece in enumerate(pieces):
            count = piece.shape[0]
            copies.append(
                pltpu.make_async_copy(piece, gathered.at[pl.ds(start, count)], sems.at[k])
            )
            start += count
        for copy in copies:
            copy.start()
        for copy in copies:
            copy.wait()

    tile_rows(turn)
    out = jnp.dot(lhs[...], gathered[...], preferred_element_type=F32).astype(BF16)
    for k, y in enumerate((y0, y1, y2, y3)):
        y[0] = out[k * BLK : k * BLK + TOP]
        zo[0, k] = out[k * BLK + TOP : (k + 1) * BLK]


def forward_blocks(table, place, vals, pieces):
    yspec = pl.BlockSpec((1, TOP, HID), lambda g, t, p: (lax.rem(g + p[0], NZ), 0, 0))
    nodes = NX * NC * BLK
    return pl.pallas_call(
        forward_kernel,
        grid_spec=pltpu.PrefetchScalarGridSpec(
            num_scalar_prefetch=2,
            grid=(NZ,),
            in_specs=[whole(NB, BLK, BLK)] + [pl.BlockSpec(memory_space=pltpu.HBM)] * len(pieces),
            out_specs=[yspec] * NY
            + [pl.BlockSpec((1, NY, BLK - TOP, HID), lambda g, t, p: (g, 0, 0, 0))],
            scratch_shapes=[
                pltpu.VMEM((nodes, HID), BF16),
                pltpu.VMEM((NY * BLK, nodes), BF16),
                pltpu.SemaphoreType.DMA((len(pieces),)),
            ],
        ),
        out_shape=[jax.ShapeDtypeStruct((NZ, TOP, HID), BF16)] * NY
        + [jax.ShapeDtypeStruct((NZ, NY, BLK - TOP, HID), BF16)],
        compiler_params=pltpu.CompilerParams(vmem_limit_bytes=16 << 20),
        name="forward_blocks",
    )(table, place, vals, *pieces)


def turn_kernel(after, vals, vals_t):
    del after
    for k in range(vals.shape[0]):
        vals_t[k] = vals[k].T


def turned(vals, after):
    group = 12
    block = pl.BlockSpec((group, BLK, BLK), lambda g: (g, 0, 0))
    return pl.pallas_call(
        turn_kernel,
        grid=(NB // group,),
        in_specs=[pl.BlockSpec(memory_space=pl.ANY), block],
        out_specs=block,
        out_shape=jax.ShapeDtypeStruct((NB, BLK, BLK), BF16),
        compiler_params=pltpu.CompilerParams(vmem_limit_bytes=4 << 20),
        name="turned",
    )(after, vals)


def backward_kernel(table, place, vals, *rest):
    pieces = rest[: NY + NZ]
    near, away, slope, acc, lhs, sems = rest[NY + NZ :]
    turn = pl.program_id(0)

    @pl.when(turn == 0)
    def _():
        lower, upper = pl.ds(0, HALF), pl.ds(HALF, HALF)
        moves = [(pieces[k], slope.at[:, k, lower]) for k in range(NY)]
        for k in range(NZ):
            moves.append((pieces[NY + k], slope.at[lax.rem(place[0] + k, NZ), :, upper]))
        copies = [
            pltpu.make_async_copy(src, dst, sems.at[k]) for k, (src, dst) in enumerate(moves)
        ]
        for copy in copies:
            copy.start()
        acc[...] = jnp.zeros_like(acc)
        for copy in copies:
            copy.wait()

    for j in range(NX * NC):
        for k in range(NY):
            slot = table[(turn * NY + k) * NX * NC + j]
            fill_tile(slot, vals, lhs, j * BLK, k * BLK)

    acc[...] += jnp.dot(
        lhs[...], slope[turn].reshape(NY * BLK, HID), preferred_element_type=F32
    )

    @pl.when(turn == NZ - 1)
    def _():
        near[...] = acc[: NX * BLK]
        away[...] = acc[NX * BLK :].astype(BF16)


def backward_blocks(table, place, vals, pieces):
    nodes = NX * NC * BLK
    return pl.pallas_call(
        backward_kernel,
        grid_spec=pltpu.PrefetchScalarGridSpec(
            num_scalar_prefetch=2,
            grid=(NZ,),
            in_specs=[whole(NB, BLK, BLK)] + [pl.BlockSpec(memory_space=pltpu.HBM)] * len(pieces),
            out_specs=[whole(NX * BLK, HID), whole(NX * BLK, HID)],
            scratch_shapes=[
                pltpu.VMEM((NZ, NY, BLK, HID), BF16),
                pltpu.VMEM((nodes, HID), F32),
                pltpu.VMEM((nodes, NY * BLK), BF16),
                pltpu.SemaphoreType.DMA((len(pieces),)),
            ],
        ),
        out_shape=[
            jax.ShapeDtypeStruct((NX * BLK, HID), F32),
            jax.ShapeDtypeStruct((NX * BLK, HID), BF16),
        ],
        compiler_params=pltpu.CompilerParams(vmem_limit_bytes=20 << 20),
        name="backward_blocks",
    )(table, place, vals, *pieces)


def slot_table(block_rows, block_cols, live):
    key = jnp.where(live, block_rows * (NX * NC) + block_cols, -1)
    shape = (NZ * NY * NX * NC, NB)
    spots = lax.broadcasted_iota(jnp.int32, shape, 0)
    slot_ids = lax.broadcasted_iota(jnp.int32, shape, 1)
    return jnp.min(jnp.where(spots == key[None, :], slot_ids, NB), axis=1)


ZGROUPS = [[k * NY + n for k in range(NZ)] for n in range(NY)]


def exchange(parts, groups):
    return lax.all_to_all(parts, "col", 0, 0, axis_index_groups=groups, tiled=True)


def spread(own, groups):
    return exchange(jnp.broadcast_to(own, (len(groups[0]), *own.shape)), groups)


def on_device(features, weight, cotangent, block_values, block_coords):
    values = block_values[0, 0]
    coords = block_coords[0, 0]
    row = lax.axis_index("row")
    col = lax.axis_index("col")
    x, core = row // NC, row % NC
    z, y = col // NY, col % NY
    place = jnp.stack([z, y]).astype(jnp.int32)

    near_x = jnp.concatenate(ring_gather(features.astype(BF16), "x", NX), 0)
    gathered = [near_x, shift(near_x, "core", 1)]

    live = coords[0] >= 0
    zr = lax.rem(coords[0] // NY - z + NZ, NZ)
    yr = lax.rem(coords[0] % NY - y + NY, NY)
    xr = lax.rem(coords[1] // NC - x + NX, NX)
    cr = lax.rem(coords[1] % NC - core + NC, NC)
    forward_table = slot_table(zr * NY + yr, cr * NX + xr, live)
    backward_table = slot_table(coords[0] // NY * NY + yr, cr * NX + xr, live)

    y0, y1, y2, y3, zo = forward_blocks(forward_table, place, values, gathered)
    values_t = turned(values, zo)
    by_y = ring_sum([y0, y1, y2, y3], "y").astype(BF16)
    by_z = ring_sum([zo[k] for k in range(NZ)], "z")
    top = exchange(by_y, ZGROUPS)
    bottom = ring_sum([by_z[k] for k in range(NY)], "y", wire=F32)
    top = jnp.sum(top.astype(F32), axis=0)
    mixed = jnp.concatenate([top, bottom], 0)

    wcopy = weight.astype(BF16)
    high = mixed.astype(BF16)
    low = (mixed - high.astype(F32)).astype(BF16)
    total = jnp.dot(high, wcopy, preferred_element_type=F32)
    total = total + jnp.dot(low, wcopy, preferred_element_type=F32)
    sigma = jax.nn.sigmoid(total)
    activated = total * sigma
    slope = cotangent.astype(F32) * sigma * (1.0 + total * (1.0 - sigma))
    slope = slope.astype(BF16)

    top_all = spread(slope[:HALF], ZGROUPS)
    bottom_all = jnp.stack(ring_gather(slope[HALF:], "y", NY))
    ypieces = ring_gather(top_all, "y", NY)
    zpieces = ring_gather(bottom_all, "z", NZ)
    pieces = ypieces + zpieces

    part, width = HID // (NX * NC), HID // (NZ * NY)
    pull = lambda left: lax.dot_general(
        slope, left, (((0,), (0,)), ((), ())), preferred_element_type=F32
    )
    local = (pull(high) + pull(low)).astype(BF16).reshape(NZ * NY, width, HID)
    shares = lax.all_to_all(local, "col", 0, 0, tiled=True)
    shares = jnp.sum(shares.astype(F32), axis=0).reshape(width, NX, NC, part)
    shares = shares.transpose(1, 2, 0, 3).reshape(NX, NC, width * part // HID, HID)
    shares = lax.dynamic_slice_in_dim(jnp.concatenate([shares, shares], 0), x, NX, 0)
    mine = lax.dynamic_index_in_dim(shares, core, 1, keepdims=False)
    other = lax.dynamic_index_in_dim(shares, 1 - core, 1, keepdims=False)
    mine = mine + shift(other, "core", 1)

    near, away = backward_blocks(backward_table, place, values_t, pieces)
    near = near + shift(away, "core", 1).astype(F32)
    spare = jnp.zeros((NX, 16 - mine.shape[1], HID), F32)
    both = jnp.concatenate([near.reshape(NX, BLK, HID), mine, spare], 1)
    sums = ring_sum([both[k] for k in range(NX)], "x", 80)
    grad = sums[:BLK].astype(BF16)
    dfeatures = lax.dot_general(
        grad, wcopy, (((1,), (1,)), ((), ())), preferred_element_type=F32
    )
    node_total = BLK * NX * NC * NZ * NY
    dweight = sums[BLK : BLK + mine.shape[1]].reshape(width, part).T * (1.0 / node_total**0.5)
    return activated, dfeatures, dweight


def solution(mesh):
    placed = (
        P(("col", "row"), None),
        P(),
        P(("row", "col"), None),
        P("row", "col", None, None, None),
        P("row", "col", None, None),
    )

    return jax.shard_map(
        on_device,
        mesh=mesh,
        in_specs=placed,
        out_specs=(P(("row", "col"), None), P(("col", "row"), None), P("row", "col")),
        check_vma=False,
    )
```

```python
import jax
import jax.numpy as jnp
from jax import lax
from jax.experimental import pallas as pl
from jax.experimental.pallas import tpu as pltpu
from jax.sharding import PartitionSpec as P

HID = 512
BLK = 128
NB = 96
NX, NC, NZ, NY = 4, 2, 8, 4
TOP = 96
PIECES = 2
F32 = jnp.float32
BF16 = jnp.bfloat16


def shift(value, axis, step):
    if axis == "z":
        return lax.ppermute(
            value, "col", [(i, (i // NY + step) % NZ * NY + i % NY) for i in range(NZ * NY)]
        )
    if axis == "y":
        return lax.ppermute(
            value, "col", [(i, i // NY * NY + (i % NY + step) % NY) for i in range(NZ * NY)]
        )
    if axis == "x":
        return lax.ppermute(
            value, "row", [(i, (i // NC + step) % NX * NC + i % NC) for i in range(NX * NC)]
        )
    return lax.ppermute(value, "row", [(i, i ^ 1) for i in range(NX * NC)])


def ring_sum(chunks, axis, cut=None, wire=BF16):
    count = len(chunks)
    far = count // 2
    cut = cut or chunks[0].shape[0] // 2

    def both_ways(right, left):
        right = shift(right.astype(wire), axis, 1).astype(F32)
        left = shift(left.astype(wire), axis, -1).astype(F32)
        return right, left

    right, left = both_ways(chunks[far][:cut], chunks[far][cut:])
    for d in range(far - 1, 0, -1):
        ahead, behind = chunks[d].astype(F32), chunks[count - d].astype(F32)
        if d == far - 1:
            ahead = jnp.concatenate([ahead[:cut] + right, ahead[cut:]], 0)
            behind = jnp.concatenate([behind[:cut], behind[cut:] + left], 0)
        else:
            ahead = ahead + right
            behind = behind + left
        right, left = both_ways(ahead, behind)
    own = chunks[0].astype(F32)
    return own + right + left


def ring_gather(own, axis, count, halves=False):
    far = count // 2
    cut = own.shape[0] // 2
    pieces = [None] * count
    pieces[0] = right = left = own
    for step in range(1, far + 1):
        last = halves and step == far
        right = shift(right[:cut] if last else right, axis, 1)
        pieces[count - step] = right
        if step < far or last:
            left = shift(left[cut:] if last else left, axis, -1)
            pieces[step] = left
    if halves:
        pieces[far : far + 1] = [right, left]
    return pieces


def fill_tile(slot, vals_ref, lhs_ref, row, col):
    tile = vals_ref[jnp.minimum(slot, NB - 1)]
    lhs_ref[pl.ds(row, BLK), pl.ds(col, BLK)] = jnp.where(
        slot < NB, tile, jnp.zeros_like(tile)
    )


def whole(*shape):
    return pl.BlockSpec(shape, lambda *_: (0,) * len(shape), pipeline_mode=pl.Buffered(1))


def forward_kernel(table, place, vals, *rest):
    pieces = rest[:PIECES]
    y0, y1, y2, y3, zo, gathered, lhs, sems = rest[PIECES:]
    turn = pl.program_id(0)

    def tile_rows(turn):
        for k in range(NY):
            for j in range(NX * NC):
                slot = table[(turn * NY + k) * NX * NC + j]
                fill_tile(slot, vals, lhs, k * BLK, j * BLK)

    @pl.when(turn == 0)
    def _():
        copies, start = [], 0
        for k, piece in enumerate(pieces):
            count = piece.shape[0]
            copies.append(
                pltpu.make_async_copy(piece, gathered.at[pl.ds(start, count)], sems.at[k])
            )
            start += count
        for copy in copies:
            copy.start()
        for copy in copies:
            copy.wait()

    tile_rows(turn)
    out = jnp.dot(lhs[...], gathered[...], preferred_element_type=F32).astype(BF16)
    for k, y in enumerate((y0, y1, y2, y3)):
        y[0] = out[k * BLK : k * BLK + TOP]
        zo[0, k] = out[k * BLK + TOP : (k + 1) * BLK]


def forward_blocks(table, place, vals, pieces):
    yspec = pl.BlockSpec((1, TOP, HID), lambda g, t, p: (lax.rem(g + p[0], NZ), 0, 0))
    nodes = NX * NC * BLK
    return pl.pallas_call(
        forward_kernel,
        grid_spec=pltpu.PrefetchScalarGridSpec(
            num_scalar_prefetch=2,
            grid=(NZ,),
            in_specs=[whole(NB, BLK, BLK)] + [pl.BlockSpec(memory_space=pltpu.HBM)] * len(pieces),
            out_specs=[yspec] * NY
            + [pl.BlockSpec(
                (1, NY, BLK - TOP, HID), lambda g, t, p: (lax.rem(g + p[0], NZ), 0, 0, 0)
            )],
            scratch_shapes=[
                pltpu.VMEM((nodes, HID), BF16),
                pltpu.VMEM((NY * BLK, nodes), BF16),
                pltpu.SemaphoreType.DMA((len(pieces),)),
            ],
        ),
        out_shape=[jax.ShapeDtypeStruct((NZ, TOP, HID), BF16)] * NY
        + [jax.ShapeDtypeStruct((NZ, NY, BLK - TOP, HID), BF16)],
        compiler_params=pltpu.CompilerParams(vmem_limit_bytes=16 << 20),
        name="forward_blocks",
    )(table, place, vals, *pieces)


def turn_kernel(after, vals, vals_t):
    del after
    for k in range(vals.shape[0]):
        vals_t[k] = vals[k].T


def turned(vals, after):
    group = 12
    block = pl.BlockSpec((group, BLK, BLK), lambda g: (g, 0, 0))
    return pl.pallas_call(
        turn_kernel,
        grid=(NB // group,),
        in_specs=[pl.BlockSpec(memory_space=pl.ANY), block],
        out_specs=block,
        out_shape=jax.ShapeDtypeStruct((NB, BLK, BLK), BF16),
        compiler_params=pltpu.CompilerParams(vmem_limit_bytes=4 << 20),
        name="turned",
    )(after, vals)


def backward_kernel(table, vals, *rest):
    pieces = rest[: NY + 2]
    near, away, slope, acc, lhs, sems = rest[NY + 2 :]
    turn = pl.program_id(0)

    @pl.when(turn == 0)
    def _():
        lower, upper = pl.ds(0, TOP), pl.ds(TOP, BLK - TOP)
        cut = NZ // 2
        y0, y1, y2a, y2b, y3, others = pieces
        moves = [
            (y0, slope.at[:, 0, lower]),
            (y1, slope.at[:, 1, lower]),
            (y2a, slope.at[pl.ds(0, cut), 2, lower]),
            (y2b, slope.at[pl.ds(cut, cut), 2, lower]),
            (y3, slope.at[:, 3, lower]),
            (others, slope.at[:, :, upper]),
        ]
        copies = [
            pltpu.make_async_copy(src, dst, sems.at[k]) for k, (src, dst) in enumerate(moves)
        ]
        for copy in copies:
            copy.start()
        acc[...] = jnp.zeros_like(acc)
        for copy in copies:
            copy.wait()

    for j in range(NX * NC):
        for k in range(NY):
            slot = table[(turn * NY + k) * NX * NC + j]
            fill_tile(slot, vals, lhs, j * BLK, k * BLK)

    acc[...] += jnp.dot(
        lhs[...], slope[turn].reshape(NY * BLK, HID), preferred_element_type=F32
    )

    @pl.when(turn == NZ - 1)
    def _():
        near[...] = acc[: NX * BLK]
        away[...] = acc[NX * BLK :].astype(BF16)


def backward_blocks(table, vals, pieces):
    nodes = NX * NC * BLK
    return pl.pallas_call(
        backward_kernel,
        grid_spec=pltpu.PrefetchScalarGridSpec(
            num_scalar_prefetch=1,
            grid=(NZ,),
            in_specs=[whole(NB, BLK, BLK)] + [pl.BlockSpec(memory_space=pltpu.HBM)] * len(pieces),
            out_specs=[whole(NX * BLK, HID), whole(NX * BLK, HID)],
            scratch_shapes=[
                pltpu.VMEM((NZ, NY, BLK, HID), BF16),
                pltpu.VMEM((nodes, HID), F32),
                pltpu.VMEM((nodes, NY * BLK), BF16),
                pltpu.SemaphoreType.DMA((len(pieces),)),
            ],
        ),
        out_shape=[
            jax.ShapeDtypeStruct((NX * BLK, HID), F32),
            jax.ShapeDtypeStruct((NX * BLK, HID), BF16),
        ],
        compiler_params=pltpu.CompilerParams(vmem_limit_bytes=20 << 20),
        name="backward_blocks",
    )(table, vals, *pieces)


def slot_table(block_rows, block_cols, live):
    key = jnp.where(live, block_rows * (NX * NC) + block_cols, -1)
    shape = (NZ * NY * NX * NC, NB)
    spots = lax.broadcasted_iota(jnp.int32, shape, 0)
    slot_ids = lax.broadcasted_iota(jnp.int32, shape, 1)
    return jnp.min(jnp.where(spots == key[None, :], slot_ids, NB), axis=1)


ZGROUPS = [[k * NY + n for k in range(NZ)] for n in range(NY)]


def exchange(parts, groups):
    return lax.all_to_all(parts, "col", 0, 0, axis_index_groups=groups, tiled=True)


def spread(own, groups):
    return exchange(jnp.broadcast_to(own, (len(groups[0]), *own.shape)), groups)


def on_device(features, weight, cotangent, block_values, block_coords):
    values = block_values[0, 0]
    coords = block_coords[0, 0]
    row = lax.axis_index("row")
    col = lax.axis_index("col")
    x, core = row // NC, row % NC
    z, y = col // NY, col % NY
    place = jnp.stack([z, y]).astype(jnp.int32)

    near_x = jnp.concatenate(ring_gather(features.astype(BF16), "x", NX), 0)
    gathered = [near_x, shift(near_x, "core", 1)]

    live = coords[0] >= 0
    zr = lax.rem(coords[0] // NY - z + NZ, NZ)
    yr = lax.rem(coords[0] % NY - y + NY, NY)
    xr = lax.rem(coords[1] // NC - x + NX, NX)
    cr = lax.rem(coords[1] % NC - core + NC, NC)
    forward_table = slot_table(zr * NY + yr, cr * NX + xr, live)
    backward_table = slot_table(coords[0] // NY * NY + yr, cr * NX + xr, live)

    y0, y1, y2, y3, zo = forward_blocks(forward_table, place, values, gathered)
    values_t = turned(values, zo)
    by_y = ring_sum([y0, y1, y2, y3], "y").astype(BF16)
    by_z = exchange(zo, ZGROUPS)
    by_z = jnp.sum(by_z.astype(F32), axis=0)
    top = exchange(by_y, ZGROUPS)
    bottom = ring_sum([by_z[k] for k in range(NY)], "y", wire=F32)
    top = jnp.sum(top.astype(F32), axis=0)
    mixed = jnp.concatenate([top, bottom], 0)

    wcopy = weight.astype(BF16)
    high = mixed.astype(BF16)
    low = (mixed - high.astype(F32)).astype(BF16)
    total = jnp.dot(high, wcopy, preferred_element_type=F32)
    total = total + jnp.dot(low, wcopy, preferred_element_type=F32)
    sigma = jax.nn.sigmoid(total)
    activated = total * sigma
    slope = cotangent.astype(F32) * sigma * (1.0 + total * (1.0 - sigma))
    slope = slope.astype(BF16)

    top_all = spread(slope[:TOP], ZGROUPS)
    bottom_all = jnp.stack(ring_gather(slope[TOP:], "y", NY))
    ypieces = ring_gather(top_all, "y", NY, halves=True)
    pieces = ypieces + [spread(bottom_all, ZGROUPS)]

    part, width = HID // (NX * NC), HID // (NZ * NY)
    pull = lambda left: lax.dot_general(
        slope, left, (((0,), (0,)), ((), ())), preferred_element_type=F32
    )
    local = (pull(high) + pull(low)).astype(BF16).reshape(NZ * NY, width, HID)
    shares = lax.all_to_all(local, "col", 0, 0, tiled=True)
    shares = jnp.sum(shares.astype(F32), axis=0).reshape(width, NX, NC, part)
    shares = shares.transpose(1, 2, 0, 3).reshape(NX, NC, width * part // HID, HID)
    shares = lax.dynamic_slice_in_dim(jnp.concatenate([shares, shares], 0), x, NX, 0)
    mine = lax.dynamic_index_in_dim(shares, core, 1, keepdims=False)
    other = lax.dynamic_index_in_dim(shares, 1 - core, 1, keepdims=False)
    mine = mine + shift(other, "core", 1)

    near, away = backward_blocks(backward_table, values_t, pieces)
    near = near + shift(away, "core", 1).astype(F32)
    spare = jnp.zeros((NX, 16 - mine.shape[1], HID), F32)
    both = jnp.concatenate([near.reshape(NX, BLK, HID), mine, spare], 1)
    sums = ring_sum([both[k] for k in range(NX)], "x", 80)
    grad = sums[:BLK].astype(BF16)
    dfeatures = lax.dot_general(
        grad, wcopy, (((1,), (1,)), ((), ())), preferred_element_type=F32
    )
    node_total = BLK * NX * NC * NZ * NY
    dweight = sums[BLK : BLK + mine.shape[1]].reshape(width, part).T * (1.0 / node_total**0.5)
    return activated, dfeatures, dweight


def solution(mesh):
    placed = (
        P(("col", "row"), None),
        P(),
        P(("row", "col"), None),
        P("row", "col", None, None, None),
        P("row", "col", None, None),
    )

    return jax.shard_map(
        on_device,
        mesh=mesh,
        in_specs=placed,
        out_specs=(P(("row", "col"), None), P(("col", "row"), None), P("row", "col")),
        check_vma=False,
    )
```

```python
import jax
import jax.numpy as jnp
from jax import lax
from jax.experimental import pallas as pl
from jax.experimental.pallas import tpu as pltpu
from jax.sharding import PartitionSpec as P

HID = 512
BLK = 128
NB = 96
NX, NC, NZ, NY = 4, 2, 8, 4
TOP = 96
NEAR = 80
PIECES = 2
F32 = jnp.float32
BF16 = jnp.bfloat16


def shift(value, axis, step):
    if axis == "z":
        return lax.ppermute(
            value, "col", [(i, (i // NY + step) % NZ * NY + i % NY) for i in range(NZ * NY)]
        )
    if axis == "y":
        return lax.ppermute(
            value, "col", [(i, i // NY * NY + (i % NY + step) % NY) for i in range(NZ * NY)]
        )
    if axis == "x":
        return lax.ppermute(
            value, "row", [(i, (i // NC + step) % NX * NC + i % NC) for i in range(NX * NC)]
        )
    return lax.ppermute(value, "row", [(i, i ^ 1) for i in range(NX * NC)])


def ring_sum(chunks, axis, cut=None, wire=BF16):
    count = len(chunks)
    far = count // 2
    cut = cut or chunks[0].shape[0] // 2

    def both_ways(right, left):
        right = shift(right.astype(wire), axis, 1).astype(F32)
        left = shift(left.astype(wire), axis, -1).astype(F32)
        return right, left

    right, left = both_ways(chunks[far][:cut], chunks[far][cut:])
    for d in range(far - 1, 0, -1):
        ahead, behind = chunks[d].astype(F32), chunks[count - d].astype(F32)
        if d == far - 1:
            ahead = jnp.concatenate([ahead[:cut] + right, ahead[cut:]], 0)
            behind = jnp.concatenate([behind[:cut], behind[cut:] + left], 0)
        else:
            ahead = ahead + right
            behind = behind + left
        right, left = both_ways(ahead, behind)
    own = chunks[0].astype(F32)
    return own + right + left


def ring_gather(own, axis, count, halves=False):
    far = count // 2
    cut = own.shape[0] // 2
    pieces = [None] * count
    pieces[0] = right = left = own
    for step in range(1, far + 1):
        last = halves and step == far
        right = shift(right[:cut] if last else right, axis, 1)
        pieces[count - step] = right
        if step < far or last:
            left = shift(left[cut:] if last else left, axis, -1)
            pieces[step] = left
    if halves:
        pieces[far : far + 1] = [right, left]
    return pieces


def fill_tile(slot, vals_ref, lhs_ref, row, col):
    tile = vals_ref[jnp.minimum(slot, NB - 1)]
    lhs_ref[pl.ds(row, BLK), pl.ds(col, BLK)] = jnp.where(
        slot < NB, tile, jnp.zeros_like(tile)
    )


def whole(*shape):
    return pl.BlockSpec(shape, lambda *_: (0,) * len(shape), pipeline_mode=pl.Buffered(1))


def forward_kernel(table, place, vals, *rest):
    pieces = rest[:PIECES]
    y0, y1, y2, y3, zo, gathered, lhs, sems = rest[PIECES:]
    turn = pl.program_id(0)

    def tile_rows(turn):
        for k in range(NY):
            for j in range(NX * NC):
                slot = table[(turn * NY + k) * NX * NC + j]
                fill_tile(slot, vals, lhs, k * BLK, j * BLK)

    @pl.when(turn == 0)
    def _():
        copies, start = [], 0
        for k, piece in enumerate(pieces):
            count = piece.shape[0]
            copies.append(
                pltpu.make_async_copy(piece, gathered.at[pl.ds(start, count)], sems.at[k])
            )
            start += count
        for copy in copies:
            copy.start()
        for copy in copies:
            copy.wait()

    tile_rows(turn)
    out = jnp.dot(lhs[...], gathered[...], preferred_element_type=F32).astype(BF16)
    for k, y in enumerate((y0, y1, y2, y3)):
        y[0] = out[k * BLK : k * BLK + TOP]
        zo[0, k] = out[k * BLK + TOP : (k + 1) * BLK]


def forward_blocks(table, place, vals, pieces):
    yspec = pl.BlockSpec((1, TOP, HID), lambda g, t, p: (lax.rem(g + p[0], NZ), 0, 0))
    nodes = NX * NC * BLK
    return pl.pallas_call(
        forward_kernel,
        grid_spec=pltpu.PrefetchScalarGridSpec(
            num_scalar_prefetch=2,
            grid=(NZ,),
            in_specs=[whole(NB, BLK, BLK)] + [pl.BlockSpec(memory_space=pltpu.HBM)] * len(pieces),
            out_specs=[yspec] * NY
            + [pl.BlockSpec(
                (1, NY, BLK - TOP, HID), lambda g, t, p: (lax.rem(g + p[0], NZ), 0, 0, 0)
            )],
            scratch_shapes=[
                pltpu.VMEM((nodes, HID), BF16),
                pltpu.VMEM((NY * BLK, nodes), BF16),
                pltpu.SemaphoreType.DMA((len(pieces),)),
            ],
        ),
        out_shape=[jax.ShapeDtypeStruct((NZ, TOP, HID), BF16)] * NY
        + [jax.ShapeDtypeStruct((NZ, NY, BLK - TOP, HID), BF16)],
        compiler_params=pltpu.CompilerParams(vmem_limit_bytes=16 << 20),
        name="forward_blocks",
    )(table, place, vals, *pieces)


def turn_kernel(after, vals, vals_t):
    del after
    for k in range(vals.shape[0]):
        vals_t[k] = vals[k].T


def turned(vals, after):
    group = 12
    block = pl.BlockSpec((group, BLK, BLK), lambda g: (g, 0, 0))
    return pl.pallas_call(
        turn_kernel,
        grid=(NB // group,),
        in_specs=[pl.BlockSpec(memory_space=pl.ANY), block],
        out_specs=block,
        out_shape=jax.ShapeDtypeStruct((NB, BLK, BLK), BF16),
        compiler_params=pltpu.CompilerParams(vmem_limit_bytes=4 << 20),
        name="turned",
    )(after, vals)


def backward_kernel(table, place, vals, *rest):
    pieces = rest[: NY + 1 + NZ]
    near, away, slope, acc, lhs, sems = rest[NY + 1 + NZ :]
    turn = pl.program_id(0)

    @pl.when(turn == 0)
    def _():
        lower, upper = pl.ds(0, NEAR), pl.ds(NEAR, BLK - NEAR)
        cut = NZ // 2
        y0, y1, y2a, y2b, y3 = pieces[: NY + 1]
        moves = [
            (y0, slope.at[:, 0, lower]),
            (y1, slope.at[:, 1, lower]),
            (y2a, slope.at[pl.ds(0, cut), 2, lower]),
            (y2b, slope.at[pl.ds(cut, cut), 2, lower]),
            (y3, slope.at[:, 3, lower]),
        ]
        for k in range(NZ):
            moves.append((pieces[NY + 1 + k], slope.at[lax.rem(place[0] + k, NZ), :, upper]))
        copies = [
            pltpu.make_async_copy(src, dst, sems.at[k]) for k, (src, dst) in enumerate(moves)
        ]
        for copy in copies:
            copy.start()
        acc[...] = jnp.zeros_like(acc)
        for copy in copies:
            copy.wait()

    for j in range(NX * NC):
        for k in range(NY):
            slot = table[(turn * NY + k) * NX * NC + j]
            fill_tile(slot, vals, lhs, j * BLK, k * BLK)

    acc[...] += jnp.dot(
        lhs[...], slope[turn].reshape(NY * BLK, HID), preferred_element_type=F32
    )

    @pl.when(turn == NZ - 1)
    def _():
        near[...] = acc[: NX * BLK]
        away[...] = acc[NX * BLK :].astype(BF16)


def backward_blocks(table, place, vals, pieces):
    nodes = NX * NC * BLK
    return pl.pallas_call(
        backward_kernel,
        grid_spec=pltpu.PrefetchScalarGridSpec(
            num_scalar_prefetch=2,
            grid=(NZ,),
            in_specs=[whole(NB, BLK, BLK)] + [pl.BlockSpec(memory_space=pltpu.HBM)] * len(pieces),
            out_specs=[whole(NX * BLK, HID), whole(NX * BLK, HID)],
            scratch_shapes=[
                pltpu.VMEM((NZ, NY, BLK, HID), BF16),
                pltpu.VMEM((nodes, HID), F32),
                pltpu.VMEM((nodes, NY * BLK), BF16),
                pltpu.SemaphoreType.DMA((len(pieces),)),
            ],
        ),
        out_shape=[
            jax.ShapeDtypeStruct((NX * BLK, HID), F32),
            jax.ShapeDtypeStruct((NX * BLK, HID), BF16),
        ],
        compiler_params=pltpu.CompilerParams(vmem_limit_bytes=20 << 20),
        name="backward_blocks",
    )(table, place, vals, *pieces)


def pull_kernel(slope, high, low, out):
    left = slope[...].T
    total = jnp.dot(left, high[...], preferred_element_type=F32)
    total += jnp.dot(left, low[...], preferred_element_type=F32)
    out[...] = total.astype(BF16)


def pulled(slope, high, low):
    return pl.pallas_call(
        pull_kernel,
        out_shape=jax.ShapeDtypeStruct((HID, HID), BF16),
        compiler_params=pltpu.CompilerParams(vmem_limit_bytes=6 << 20),
        name="pulled",
    )(slope, high, low)


def slot_table(block_rows, block_cols, live):
    key = jnp.where(live, block_rows * (NX * NC) + block_cols, -1)
    shape = (NZ * NY * NX * NC, NB)
    spots = lax.broadcasted_iota(jnp.int32, shape, 0)
    slot_ids = lax.broadcasted_iota(jnp.int32, shape, 1)
    return jnp.min(jnp.where(spots == key[None, :], slot_ids, NB), axis=1)


ZGROUPS = [[k * NY + n for k in range(NZ)] for n in range(NY)]


def exchange(parts, groups):
    return lax.all_to_all(parts, "col", 0, 0, axis_index_groups=groups, tiled=True)


def spread(own, groups):
    return exchange(jnp.broadcast_to(own, (len(groups[0]), *own.shape)), groups)


def on_device(features, weight, cotangent, block_values, block_coords):
    values = block_values[0, 0]
    coords = block_coords[0, 0]
    row = lax.axis_index("row")
    col = lax.axis_index("col")
    x, core = row // NC, row % NC
    z, y = col // NY, col % NY
    place = jnp.stack([z, y]).astype(jnp.int32)

    near_x = jnp.concatenate(ring_gather(features.astype(BF16), "x", NX), 0)
    gathered = [near_x, shift(near_x, "core", 1)]

    live = coords[0] >= 0
    zr = lax.rem(coords[0] // NY - z + NZ, NZ)
    yr = lax.rem(coords[0] % NY - y + NY, NY)
    xr = lax.rem(coords[1] // NC - x + NX, NX)
    cr = lax.rem(coords[1] % NC - core + NC, NC)
    forward_table = slot_table(zr * NY + yr, cr * NX + xr, live)
    backward_table = slot_table(coords[0] // NY * NY + yr, cr * NX + xr, live)

    y0, y1, y2, y3, zo = forward_blocks(forward_table, place, values, gathered)
    values_t = turned(values, zo)
    by_y = ring_sum([y0, y1, y2, y3], "y").astype(BF16)
    by_z = exchange(zo, ZGROUPS)
    by_z = jnp.sum(by_z.astype(F32), axis=0)
    top = exchange(by_y, ZGROUPS)
    bottom = ring_sum([by_z[k] for k in range(NY)], "y", wire=F32)
    top = jnp.sum(top.astype(F32), axis=0)
    mixed = jnp.concatenate([top, bottom], 0)

    wcopy = weight.astype(BF16)
    high = mixed.astype(BF16)
    low = (mixed - high.astype(F32)).astype(BF16)
    total = jnp.dot(high, wcopy, preferred_element_type=F32)
    total = total + jnp.dot(low, wcopy, preferred_element_type=F32)
    sigma = jax.nn.sigmoid(total)
    activated = total * sigma
    slope = cotangent.astype(F32) * sigma * (1.0 + total * (1.0 - sigma))
    slope = slope.astype(BF16)

    top_all = spread(slope[:NEAR], ZGROUPS)
    bottom_all = jnp.stack(ring_gather(slope[NEAR:], "y", NY))
    ypieces = ring_gather(top_all, "y", NY, halves=True)
    pieces = ypieces + ring_gather(bottom_all, "z", NZ)

    part, width = HID // (NX * NC), HID // (NZ * NY)
    local = pulled(slope, high, low).reshape(NZ * NY, width, HID)
    shares = lax.all_to_all(local, "col", 0, 0, tiled=True)
    shares = jnp.sum(shares.astype(F32), axis=0).reshape(width, NX, NC, part)
    shares = shares.transpose(1, 2, 0, 3).reshape(NX, NC, width * part // HID, HID)
    shares = lax.dynamic_slice_in_dim(jnp.concatenate([shares, shares], 0), x, NX, 0)
    mine = lax.dynamic_index_in_dim(shares, core, 1, keepdims=False)
    other = lax.dynamic_index_in_dim(shares, 1 - core, 1, keepdims=False)
    mine = mine + shift(other, "core", 1)

    near, away = backward_blocks(backward_table, place, values_t, pieces)
    near = near + shift(away, "core", 1).astype(F32)
    spare = jnp.zeros((NX, 16 - mine.shape[1], HID), F32)
    both = jnp.concatenate([near.reshape(NX, BLK, HID), mine, spare], 1)
    sums = ring_sum([both[k] for k in range(NX)], "x", 80)
    grad = sums[:BLK].astype(BF16)
    dfeatures = lax.dot_general(
        grad, wcopy, (((1,), (1,)), ((), ())), preferred_element_type=F32
    )
    node_total = BLK * NX * NC * NZ * NY
    dweight = sums[BLK : BLK + mine.shape[1]].reshape(width, part).T * (1.0 / node_total**0.5)
    return activated, dfeatures, dweight


def solution(mesh):
    placed = (
        P(("col", "row"), None),
        P(),
        P(("row", "col"), None),
        P("row", "col", None, None, None),
        P("row", "col", None, None),
    )

    return jax.shard_map(
        on_device,
        mesh=mesh,
        in_specs=placed,
        out_specs=(P(("row", "col"), None), P(("col", "row"), None), P("row", "col")),
        check_vma=False,
    )
```

```python
import jax
import jax.numpy as jnp
from jax import lax
from jax.experimental import pallas as pl
from jax.experimental.pallas import tpu as pltpu
from jax.sharding import PartitionSpec as P

HID = 512
BLK = 128
NB = 96
NX, NC, NZ, NY = 4, 2, 8, 4
TOP = 96
NEAR = 80
PIECES = 2
F32 = jnp.float32
BF16 = jnp.bfloat16


def shift(value, axis, step):
    if axis == "z":
        return lax.ppermute(
            value, "col", [(i, (i // NY + step) % NZ * NY + i % NY) for i in range(NZ * NY)]
        )
    if axis == "y":
        return lax.ppermute(
            value, "col", [(i, i // NY * NY + (i % NY + step) % NY) for i in range(NZ * NY)]
        )
    if axis == "x":
        return lax.ppermute(
            value, "row", [(i, (i // NC + step) % NX * NC + i % NC) for i in range(NX * NC)]
        )
    return lax.ppermute(value, "row", [(i, i ^ 1) for i in range(NX * NC)])


def ring_sum(chunks, axis, cut=None, wire=BF16):
    count = len(chunks)
    far = count // 2
    cut = cut or chunks[0].shape[0] // 2

    def both_ways(right, left):
        right = shift(right.astype(wire), axis, 1).astype(F32)
        left = shift(left.astype(wire), axis, -1).astype(F32)
        return right, left

    right, left = both_ways(chunks[far][:cut], chunks[far][cut:])
    for d in range(far - 1, 0, -1):
        ahead, behind = chunks[d].astype(F32), chunks[count - d].astype(F32)
        if d == far - 1:
            ahead = jnp.concatenate([ahead[:cut] + right, ahead[cut:]], 0)
            behind = jnp.concatenate([behind[:cut], behind[cut:] + left], 0)
        else:
            ahead = ahead + right
            behind = behind + left
        right, left = both_ways(ahead, behind)
    own = chunks[0].astype(F32)
    return own + right + left


def ring_gather(own, axis, count, halves=False):
    far = count // 2
    cut = own.shape[0] // 2
    pieces = [None] * count
    pieces[0] = right = left = own
    for step in range(1, far + 1):
        last = halves and step == far
        right = shift(right[:cut] if last else right, axis, 1)
        pieces[count - step] = right
        if step < far or last:
            left = shift(left[cut:] if last else left, axis, -1)
            pieces[step] = left
    if halves:
        pieces[far : far + 1] = [right, left]
    return pieces


def fill_tile(slot, vals_ref, lhs_ref, row, col):
    tile = vals_ref[jnp.minimum(slot, NB - 1)]
    lhs_ref[pl.ds(row, BLK), pl.ds(col, BLK)] = jnp.where(
        slot < NB, tile, jnp.zeros_like(tile)
    )


def whole(*shape):
    return pl.BlockSpec(shape, lambda *_: (0,) * len(shape), pipeline_mode=pl.Buffered(1))


def fill_rows(table, turn, vals, lhs):
    for k in range(NY):
        for j in range(NX * NC):
            fill_tile(table[(turn * NY + k) * NX * NC + j], vals, lhs, k * BLK, j * BLK)


def fill_columns(table, turn, vals, lhs):
    for j in range(NX * NC):
        for k in range(NY):
            fill_tile(table[(turn * NY + k) * NX * NC + j], vals, lhs, j * BLK, k * BLK)


def in_turns(table, vals, fill, tiles, multiply):
    turn = pl.program_id(0) * 2
    fill(table, turn + 1, vals, tiles[1])
    multiply(turn, 0, tiles[0])
    fill(table, jnp.minimum(turn + 2, NZ - 1), vals, tiles[0])
    multiply(turn + 1, 1, tiles[1])


def forward_kernel(table, vals, *rest):
    pieces = rest[:PIECES]
    y0, y1, y2, y3, zo, gathered, even, odd, sems = rest[PIECES:]

    @pl.when(pl.program_id(0) == 0)
    def _():
        copies, start = [], 0
        for k, piece in enumerate(pieces):
            count = piece.shape[0]
            copies.append(
                pltpu.make_async_copy(piece, gathered.at[pl.ds(start, count)], sems.at[k])
            )
            start += count
        for copy in copies:
            copy.start()
        fill_rows(table, 0, vals, even)
        for copy in copies:
            copy.wait()

    def multiply(turn, n, lhs):
        out = jnp.dot(lhs[...], gathered[...], preferred_element_type=F32).astype(BF16)
        for k, y in enumerate((y0, y1, y2, y3)):
            y[n] = out[k * BLK : k * BLK + TOP]
            zo[n, k] = out[k * BLK + TOP : (k + 1) * BLK]

    in_turns(table, vals, fill_rows, (even, odd), multiply)


def forward_blocks(table, vals, pieces):
    nodes = NX * NC * BLK
    return pl.pallas_call(
        forward_kernel,
        grid_spec=pltpu.PrefetchScalarGridSpec(
            num_scalar_prefetch=1,
            grid=(NZ // 2,),
            in_specs=[whole(NB, BLK, BLK)] + [pl.BlockSpec(memory_space=pltpu.HBM)] * len(pieces),
            out_specs=[pl.BlockSpec((2, TOP, HID), lambda g, t: (g, 0, 0))] * NY
            + [pl.BlockSpec((2, NY, BLK - TOP, HID), lambda g, t: (g, 0, 0, 0))],
            scratch_shapes=[
                pltpu.VMEM((nodes, HID), BF16),
                pltpu.VMEM((NY * BLK, nodes), BF16),
                pltpu.VMEM((NY * BLK, nodes), BF16),
                pltpu.SemaphoreType.DMA((len(pieces),)),
            ],
        ),
        out_shape=[jax.ShapeDtypeStruct((NZ, TOP, HID), BF16)] * NY
        + [jax.ShapeDtypeStruct((NZ, NY, BLK - TOP, HID), BF16)],
        compiler_params=pltpu.CompilerParams(vmem_limit_bytes=20 << 20),
        name="forward_blocks",
    )(table, vals, *pieces)


def turn_kernel(after, vals, vals_t):
    del after
    for k in range(vals.shape[0]):
        vals_t[k] = vals[k].T


def turned(vals, after):
    group = 12
    block = pl.BlockSpec((group, BLK, BLK), lambda g: (g, 0, 0))
    return pl.pallas_call(
        turn_kernel,
        grid=(NB // group,),
        in_specs=[pl.BlockSpec(memory_space=pl.ANY), block],
        out_specs=block,
        out_shape=jax.ShapeDtypeStruct((NB, BLK, BLK), BF16),
        compiler_params=pltpu.CompilerParams(vmem_limit_bytes=4 << 20),
        name="turned",
    )(after, vals)


def backward_kernel(table, place, vals, *rest):
    pieces = rest[: NY + 1 + NZ]
    near, away, slope, acc, even, odd, sems = rest[NY + 1 + NZ :]

    @pl.when(pl.program_id(0) == 0)
    def _():
        lower, upper = pl.ds(0, NEAR), pl.ds(NEAR, BLK - NEAR)
        cut = NZ // 2
        y0, y1, y2a, y2b, y3 = pieces[: NY + 1]
        moves = [
            (y0, slope.at[:, 0, lower]),
            (y1, slope.at[:, 1, lower]),
            (y2a, slope.at[pl.ds(0, cut), 2, lower]),
            (y2b, slope.at[pl.ds(cut, cut), 2, lower]),
            (y3, slope.at[:, 3, lower]),
        ]
        for k in range(NZ):
            moves.append((pieces[NY + 1 + k], slope.at[lax.rem(place[0] + k, NZ), :, upper]))
        copies = [
            pltpu.make_async_copy(src, dst, sems.at[k]) for k, (src, dst) in enumerate(moves)
        ]
        for copy in copies:
            copy.start()
        acc[...] = jnp.zeros_like(acc)
        fill_columns(table, 0, vals, even)
        for copy in copies:
            copy.wait()

    def multiply(turn, n, lhs):
        acc[...] += jnp.dot(
            lhs[...], slope[turn].reshape(NY * BLK, HID), preferred_element_type=F32
        )

    in_turns(table, vals, fill_columns, (even, odd), multiply)

    @pl.when(pl.program_id(0) == NZ // 2 - 1)
    def _():
        near[...] = acc[: NX * BLK]
        away[...] = acc[NX * BLK :].astype(BF16)


def backward_blocks(table, place, vals, pieces):
    nodes = NX * NC * BLK
    return pl.pallas_call(
        backward_kernel,
        grid_spec=pltpu.PrefetchScalarGridSpec(
            num_scalar_prefetch=2,
            grid=(NZ // 2,),
            in_specs=[whole(NB, BLK, BLK)] + [pl.BlockSpec(memory_space=pltpu.HBM)] * len(pieces),
            out_specs=[whole(NX * BLK, HID), whole(NX * BLK, HID)],
            scratch_shapes=[
                pltpu.VMEM((NZ, NY, BLK, HID), BF16),
                pltpu.VMEM((nodes, HID), F32),
                pltpu.VMEM((nodes, NY * BLK), BF16),
                pltpu.VMEM((nodes, NY * BLK), BF16),
                pltpu.SemaphoreType.DMA((len(pieces),)),
            ],
        ),
        out_shape=[
            jax.ShapeDtypeStruct((NX * BLK, HID), F32),
            jax.ShapeDtypeStruct((NX * BLK, HID), BF16),
        ],
        compiler_params=pltpu.CompilerParams(vmem_limit_bytes=20 << 20),
        name="backward_blocks",
    )(table, place, vals, *pieces)


def pull_kernel(slope, high, low, out):
    left = slope[...].T
    total = jnp.dot(left, high[...], preferred_element_type=F32)
    total += jnp.dot(left, low[...], preferred_element_type=F32)
    out[...] = total.astype(BF16)


def pulled(slope, high, low):
    return pl.pallas_call(
        pull_kernel,
        out_shape=jax.ShapeDtypeStruct((HID, HID), BF16),
        compiler_params=pltpu.CompilerParams(vmem_limit_bytes=6 << 20),
        name="pulled",
    )(slope, high, low)


def slot_table(block_rows, block_cols, live):
    key = jnp.where(live, block_rows * (NX * NC) + block_cols, -1)
    shape = (NZ * NY * NX * NC, NB)
    spots = lax.broadcasted_iota(jnp.int32, shape, 0)
    slot_ids = lax.broadcasted_iota(jnp.int32, shape, 1)
    return jnp.min(jnp.where(spots == key[None, :], slot_ids, NB), axis=1)


ZGROUPS = [[k * NY + n for k in range(NZ)] for n in range(NY)]


def exchange(parts, groups):
    return lax.all_to_all(parts, "col", 0, 0, axis_index_groups=groups, tiled=True)


def spread(own, groups):
    return exchange(jnp.broadcast_to(own, (len(groups[0]), *own.shape)), groups)


def on_device(features, weight, cotangent, block_values, block_coords):
    values = block_values[0, 0]
    coords = block_coords[0, 0]
    row = lax.axis_index("row")
    col = lax.axis_index("col")
    x, core = row // NC, row % NC
    z, y = col // NY, col % NY
    place = jnp.stack([z, y]).astype(jnp.int32)

    near_x = jnp.concatenate(ring_gather(features.astype(BF16), "x", NX), 0)
    gathered = [near_x, shift(near_x, "core", 1)]

    live = coords[0] >= 0
    yr = lax.rem(coords[0] % NY - y + NY, NY)
    xr = lax.rem(coords[1] // NC - x + NX, NX)
    cr = lax.rem(coords[1] % NC - core + NC, NC)
    table = slot_table(coords[0] // NY * NY + yr, cr * NX + xr, live)

    y0, y1, y2, y3, zo = forward_blocks(table, values, gathered)
    values_t = turned(values, zo)
    by_y = ring_sum([y0, y1, y2, y3], "y").astype(BF16)
    by_z = exchange(zo, ZGROUPS)
    by_z = jnp.sum(by_z.astype(F32), axis=0)
    top = exchange(by_y, ZGROUPS)
    bottom = ring_sum([by_z[k] for k in range(NY)], "y", wire=F32)
    top = jnp.sum(top.astype(F32), axis=0)
    mixed = jnp.concatenate([top, bottom], 0)

    wcopy = weight.astype(BF16)
    high = mixed.astype(BF16)
    low = (mixed - high.astype(F32)).astype(BF16)
    total = jnp.dot(high, wcopy, preferred_element_type=F32)
    total = total + jnp.dot(low, wcopy, preferred_element_type=F32)
    sigma = jax.nn.sigmoid(total)
    activated = total * sigma
    slope = cotangent.astype(F32) * sigma * (1.0 + total * (1.0 - sigma))
    slope = slope.astype(BF16)

    top_all = spread(slope[:NEAR], ZGROUPS)
    bottom_all = jnp.stack(ring_gather(slope[NEAR:], "y", NY))
    ypieces = ring_gather(top_all, "y", NY, halves=True)
    pieces = ypieces + ring_gather(bottom_all, "z", NZ)

    part, width = HID // (NX * NC), HID // (NZ * NY)
    local = pulled(slope, high, low).reshape(NZ * NY, width, HID)
    shares = lax.all_to_all(local, "col", 0, 0, tiled=True)
    shares = jnp.sum(shares.astype(F32), axis=0).reshape(width, NX, NC, part)
    shares = shares.transpose(1, 2, 0, 3).reshape(NX, NC, width * part // HID, HID)
    shares = lax.dynamic_slice_in_dim(jnp.concatenate([shares, shares], 0), x, NX, 0)
    mine = lax.dynamic_index_in_dim(shares, core, 1, keepdims=False)
    other = lax.dynamic_index_in_dim(shares, 1 - core, 1, keepdims=False)
    mine = mine + shift(other, "core", 1)

    near, away = backward_blocks(table, place, values_t, pieces)
    near = near + shift(away, "core", 1).astype(F32)
    spare = jnp.zeros((NX, 16 - mine.shape[1], HID), F32)
    both = jnp.concatenate([near.reshape(NX, BLK, HID), mine, spare], 1)
    sums = ring_sum([both[k] for k in range(NX)], "x", 80)
    grad = sums[:BLK].astype(BF16)
    dfeatures = lax.dot_general(
        grad, wcopy, (((1,), (1,)), ((), ())), preferred_element_type=F32
    )
    node_total = BLK * NX * NC * NZ * NY
    dweight = sums[BLK : BLK + mine.shape[1]].reshape(width, part).T * (1.0 / node_total**0.5)
    return activated, dfeatures, dweight


def solution(mesh):
    placed = (
        P(("col", "row"), None),
        P(),
        P(("row", "col"), None),
        P("row", "col", None, None, None),
        P("row", "col", None, None),
    )

    return jax.shard_map(
        on_device,
        mesh=mesh,
        in_specs=placed,
        out_specs=(P(("row", "col"), None), P(("col", "row"), None), P("row", "col")),
        check_vma=False,
    )
```
